256 devices in a mesh: seq: 64 (over x, z, core), head: 4 (over y).
Axes of the slice: x: 4, y: 4, z: 8, core: 2. Of those that a mesh axis runs over, the one named last changes fastest.
Arguments:
- queries: bfloat16 [32768, 4096], P('seq', 'head'), may hold values from -6 to 6
- key_input: bfloat16 [32768, 4096], P('seq', 'head'), may hold values from -6 to 6
- value_input: bfloat16 [32768, 4096], P('seq', 'head'), may hold values from -40 to 40
- gate_input: bfloat16 [32768, 4096], P('seq', 'head'), may hold values from -8 to 8
- kv_state: float32 [32, 128, 128], P('head'), may hold values from -512 to 512
- norm_gain: float32 [4096], replicated, may hold values from 0.25 to 1.75
- out_weight: bfloat16 [4096, 4096], P('head', 'seq'), may hold values from -0.09375 to 0.09375
Outputs:
- output: bfloat16 [32768, 4096], P(('seq', 'head'))
The draws below stay inside these ranges and needn't reach their ends.
All inputs are finite; a program needn't handle non-finite values.
Results may differ from the reference program's by a relative error of at most 0.02.
Values may be sent and summed in bfloat16 or wider, within the bound.
A program may use at most 128 MiB of HBM per device.

```python
import jax
import jax.numpy as jnp
from jax import lax

H = 32
DH = 128
HD = 4096
D = 4096
BLOCK = 512
TOK_DEV = 512
TOKENS = 32768
N_HEAD = 4


def draw_value_input(key, part):
    key_base, key_cols, key_rows = jax.random.split(jax.random.fold_in(key, 7), 3)
    base = jnp.clip(jax.random.normal(key_base, (TOKENS, HD), jnp.float32), -4.0, 4.0)
    col_scale = jnp.exp(jax.random.uniform(key_cols, (1, HD), jnp.float32) * jnp.log(10.0))
    row_scale = jnp.exp(jax.random.uniform(key_rows, (TOKENS, 1), jnp.float32) * jnp.log(10.0))
    values = base * col_scale * row_scale / 10.0
    return values.astype(jnp.bfloat16)


def block_levels(own_key, extent, cuts, least, largest):
    def one(position, shards_of):
        draws = jax.random.uniform(jax.random.fold_in(jax.random.fold_in(own_key, 6), position), (shards_of,), jnp.float32, least / len(cuts), largest / len(cuts))
        return jnp.repeat(jnp.exp(draws), extent[position] // shards_of).reshape((-1,) + (1,) * (len(extent) - position - 1))

    factor_of = one(*cuts[0])
    for cut in cuts[1:]:
        factor_of = factor_of * one(*cut)
    return factor_of


def normal_values(key, shape, width, limit, cuts=(), held_as=jnp.bfloat16):
    loudness = block_levels(key, shape, cuts, -0.22, 0.18) if cuts else 1.0
    drawn = jax.random.normal(key, shape, jnp.float32) * width * loudness
    return jnp.minimum(jnp.maximum(drawn, -limit), limit).astype(held_as)


def setup_inputs(seed: int = 0) -> dict:
    seeds = jax.random.split(jax.random.key(seed), 8)
    return {
        "queries": normal_values(seeds[0], (TOKENS, HD), 1.0, 6.0, ((0, 64), (1, 4))),
        "key_input": normal_values(seeds[1], (TOKENS, HD), 1.0, 6.0, ((0, 64), (1, 4))),
        "value_input": draw_value_input(jax.random.fold_in(seeds[7], 71), 0),
        "gate_input": normal_values(seeds[3], (TOKENS, HD), 1.5, 8.0, ((0, 64), (1, 4))),
        "kv_state": normal_values(seeds[4], (H, DH, DH), (4 * TOK_DEV ** 0.5), 512.0, ((0, 4),), jnp.float32),
        "norm_gain": jnp.clip(1.0 + 0.15 * jax.random.normal(seeds[5], (HD,), jnp.float32), 0.25, 1.75),
        "out_weight": normal_values(seeds[6], (HD, D), HD ** -0.5, 0.09375, ((0, 4), (1, 64))),
    }


epsilon = 1e-05

def reference(queries, key_input, value_input, gate_input, kv_state, norm_gain, out_weight):
    num_blocks = TOKENS // BLOCK
    q_blocks = queries.reshape(num_blocks, BLOCK, H, DH)
    k_blocks = key_input.reshape(num_blocks, BLOCK, H, DH)
    v_blocks = value_input.reshape(num_blocks, BLOCK, H, DH)
    causal = jnp.arange(BLOCK)[:, None] >= jnp.arange(BLOCK)[None, :]
    highest = lax.Precision.HIGHEST

    def advance(state, blocks):
        q_rows, k_rows, v_rows = blocks
        q_float = q_rows.astype(jnp.float32)
        k_float = k_rows.astype(jnp.float32)
        v_float = v_rows.astype(jnp.float32)
        carried_part = jnp.einsum('thd,hde->the', q_float, state, precision=highest)
        scores = jnp.einsum('thd,shd->hts', q_float, k_float, precision=highest)
        scores = jnp.where(causal[None], scores, 0.0).astype(jnp.bfloat16)
        scores = lax.optimization_barrier(scores).astype(jnp.float32)
        inner_part = jnp.einsum('hts,she->the', scores, v_float, precision=highest)
        new_state = state + jnp.einsum('thd,the->hde', k_float, v_float, precision=highest)
        return (new_state, (carried_part + inner_part).astype(jnp.bfloat16))
    final_state, attn = lax.scan(advance, kv_state.astype(jnp.float32), (q_blocks, k_blocks, v_blocks))
    attn_float = attn.reshape(TOKENS, HD).astype(jnp.float32)
    mean_square = lax.optimization_barrier(jnp.mean(attn_float * attn_float, axis=1, keepdims=True))
    hidden = attn_float * lax.rsqrt(mean_square + epsilon) * norm_gain[None, :]
    hidden = (hidden * jax.nn.sigmoid(gate_input.astype(jnp.float32))).astype(jnp.bfloat16)
    group = HD // N_HEAD
    hidden_blocks = hidden.reshape(num_blocks, BLOCK, HD)

    def project(rows):
        summed = jnp.zeros((BLOCK, D), jnp.float32)
        for index in range(N_HEAD):
            partial_rows = jnp.dot(rows[:, index * group:(index + 1) * group], out_weight[index * group:(index + 1) * group], preferred_element_type=jnp.float32).astype(jnp.bfloat16)
            summed = summed + lax.optimization_barrier(partial_rows).astype(jnp.float32)
        return summed.astype(jnp.bfloat16)
    return lax.map(project, hidden_blocks).reshape(TOKENS, D)
```

```python
import jax
import jax.numpy as jnp
from jax import lax
from jax.experimental import pallas as pl
from jax.experimental.pallas import tpu as pltpu
from jax.sharding import PartitionSpec as P

MESH = pl.DeviceIdType.MESH
DH = 128
X, Z, Y = 4, 8, 4
EPS = 1e-05
F32, BF16 = jnp.float32, jnp.bfloat16


def dot(a, b, ca, cb):
    return lax.dot_general(a, b, (((ca,), (cb,)), ((), ())), preferred_element_type=F32)


def body(
    q_hbm, k_hbm, v_hbm, g_hbm, kv_hbm, gain_ref, w_hbm, out_ref,
    q, k, v, g, kv, w, wt,
    s_own, s_other, t_send, t_recv, line, l_send, l_recv, p_send, p_chip, c_send, c_recv,
    inner, gated, hidden, sq, sq_recv, terms,
    ra_p, ra_m, rb_p, rb_m, rc_p, rc_m,
    load, wz_s, wz_r, wx_s, wx_r, wc_s, wc_r,
    sc_s, sc_r, tz_s, tz_r, lx_s, lx_r, pz_s, pz_r, cc_s, cc_r, sq_s, sq_r,
    rs_s, rs_r,
):
    seq, y = lax.axis_index("seq"), lax.axis_index("head")
    c = lax.rem(seq, 2)
    chip = seq // 2
    z = lax.rem(chip, Z)
    x = chip // Z

    def at(xx, zz, cc):
        return {"seq": (lax.rem(xx + X, X) * Z + lax.rem(zz + Z, Z)) * 2 + cc}

    def row(step):
        return {"head": lax.rem(y + step + Y, Y)}

    partner = at(x, z, 1 - c)
    y_quarter = [pl.ds(pl.multiple_of(lax.rem(y + d, Y) * 128, 128), 128) for d in range(Y)]

    loads = [(w_hbm, w), (k_hbm, k), (v_hbm, v), (q_hbm, q), (kv_hbm, kv), (g_hbm, g)]
    copies = [pltpu.make_async_copy(a, b, load.at[i]) for i, (a, b) in enumerate(loads)]
    for copy in copies:
        copy.start()
    barrier = pltpu.get_barrier_semaphore()
    partners = [partner] + [at(x, z + d, c) for d in range(1, Z)] + [at(x + d, z, c) for d in range(1, X)]
    partners += [row(d) for d in range(1, Y)]
    for device in partners:
        pl.semaphore_signal(barrier, inc=1, device_id=device, device_id_type=MESH)
    copies[0].wait()
    eye = (
        lax.broadcasted_iota(jnp.int32, (64, 64), 0) == lax.broadcasted_iota(jnp.int32, (64, 64), 1)
    ).astype(F32).astype(BF16)
    wt[0, 0, c] = dot(eye, w[...], 1, 1).astype(BF16)
    pl.semaphore_wait(barrier, len(partners))

    def remote(src, dst, ssem, rsem, device):
        return pltpu.make_async_remote_copy(
            src_ref=src, dst_ref=dst, send_sem=ssem, recv_sem=rsem, device_id=device, device_id_type=MESH
        )

    def wz(src, dst):
        step = 1 if dst % 2 else -1
        return remote(wt.at[src, 0, c], wt.at[dst, 0, c], wz_s.at[dst], wz_r.at[dst], at(x, z + step, c))

    def wx(j, kind):
        step = 1 if kind % 2 == 0 else -1
        if kind < 2:
            src, dst = wt.at[j, 0, c], wt.at[j, 1 + kind, c]
        else:
            half = pl.ds(32 * (kind - 2), 32)
            src, dst = wt.at[j, kind - 1, c, half], wt.at[j, 3, c, half]
        return remote(src, dst, wx_s.at[j, kind], wx_r.at[j, kind], at(x + step, z, c))

    def wc(j, place):
        block = wt.at[j, place, c]
        return remote(block, block, wc_s.at[j, place], wc_r.at[j, place], partner)

    def spread(j):
        wx(j, 0).start()
        wx(j, 1).start()
        wc(j, 0).start()

    def service_z(s):
        a = 2 * s - 1
        wz(max(a - 2, 0), a).wait_recv()
        if s < 4:
            wz(a, a + 2).start()
        spread(a)
        if s < 4:
            wz(max(a - 1, 0), a + 1).wait_recv()
            if s < 3:
                wz(a + 1, a + 3).start()
            spread(a + 1)

    def service_x(j):
        wx(j, 0).wait_recv()
        wx(j, 2).start()
        wx(j, 1).wait_recv()
        wx(j, 3).start()
        wc(j, 1).start()
        wc(j, 2).start()

    def service_far(j):
        wx(j, 2).wait_recv()
        wx(j, 3).wait_recv()
        wc(j, 3).start()

    wz(0, 1).start()
    wz(0, 2).start()
    spread(0)

    copies[1].wait()
    copies[2].wait()
    for h in range(8):
        cols = slice(h * DH, (h + 1) * DH)
        s_own[h // 4, h % 4] = dot(k[:, cols], v[:, cols], 0, 0)
    state_swap = remote(s_own.at[1 - c], s_other, sc_s, sc_r, partner)
    state_swap.start()

    copies[3].wait()
    lower = lax.broadcasted_iota(jnp.int32, (256, 256), 0) >= lax.broadcasted_iota(jnp.int32, (256, 256), 1)

    def local(h):
        cols = slice(h * DH, (h + 1) * DH)
        for r in range(2):
            rows = slice(r * 256, (r + 1) * 256)
            q_rows = q[rows, cols]
            near = jnp.where(lower, dot(q_rows, k[rows, cols], 1, 1), 0.0).astype(BF16)
            total = dot(near, v[rows, cols], 1, 0)
            if r == 1:
                far = dot(q_rows, k[0:256, cols], 1, 1).astype(BF16)
                total = total + dot(far, v[0:256, cols], 1, 0)
            inner[rows, cols] = total

    local(0)
    state_swap.wait_recv()
    for h in range(4):
        t = (s_own[c, h] + s_other[h]).astype(BF16)
        t_send[2 * h] = t[0:64]
        t_send[2 * h + 1] = t[64:128]

    def tz(d):
        to = lax.rem(z + d, Z)
        return remote(t_send.at[to], t_recv.at[z], tz_s.at[d], tz_r.at[d], at(x, z + d, c))

    def pz(d):
        to = lax.rem(z + d, Z)
        return remote(p_send.at[to], p_chip.at[z], pz_s.at[d], pz_r.at[d], at(x, z + d, c))

    def lx(d):
        return remote(l_send, l_recv.at[d], lx_s.at[d], lx_r.at[d], at(x + d, z, c))

    for d in (4, 3, 5, 2, 6, 1, 7):
        tz(d).start()
    t_recv[z] = t_send[z]
    service_z(1)
    local(1)
    local(2)
    local(3)
    for d in range(1, Z):
        tz(d).wait_recv()
    total = jnp.zeros((64, DH), F32)
    for i in range(Z):
        line[i] = total
        total = total + t_recv[i].astype(F32)
    l_send[...] = total.astype(BF16)
    for d in (2, 1, 3):
        lx(d).start()
    service_z(2)
    service_x(0)
    local(4)
    for d in range(1, X):
        lx(d).wait_recv()
    before = jnp.zeros((64, DH), F32)
    for d in range(1, X):
        before = before + jnp.where(x >= d, l_recv[d].astype(F32), 0.0)
    for i in range(Z):
        p_send[i] = (line[i] + before).astype(BF16)
    for d in (4, 3, 5, 2, 6, 1, 7):
        pz(d).start()
    p_chip[z] = p_send[z]
    service_z(3)
    local(5)
    local(6)
    local(7)
    service_x(1)
    service_far(0)
    copies[5].wait()
    for i in range(4):
        rows = slice(i * 128, (i + 1) * 128)
        gated[rows] = gain_ref[...] * jax.nn.sigmoid(g[rows].astype(F32))
    service_z(4)
    copies[4].wait()
    for d in range(1, Z):
        pz(d).wait_recv()
    own_part = (1 - c).astype(F32)
    other_part = c.astype(F32)
    for h in range(4):
        base = jnp.concatenate([p_chip[2 * h].astype(F32), p_chip[2 * h + 1].astype(F32)], axis=0)
        c_send[h] = base + own_part * s_own[c, h]
        s_other[h] = base + other_part * s_other[h]
    prefix_swap = remote(c_send, c_recv, cc_s, cc_r, partner)
    prefix_swap.start()

    def carried(h, state):
        hi = state.astype(BF16)
        lo = (state - hi.astype(F32)).astype(BF16)
        return jnp.concatenate([hi, lo], axis=0)

    def finish(half, first):
        prefix = s_other if half == 0 else c_recv
        which = c if half == 0 else 1 - c
        for h in range(4):
            state = carried(h, kv[which * 4 + h] + prefix[h])
            cols = pl.ds(pl.multiple_of((which * 4 + h) * DH, DH), DH)
            qq = q[:, cols]
            attn = inner[:, cols] + dot(jnp.concatenate([qq, qq], axis=1), state, 1, 0)
            attn = attn.astype(BF16).astype(F32)
            square = attn * attn
            if first and h == 0:
                sq[...] = square
            else:
                sq[...] += square
            hidden[:, cols] = (attn * gated[:, cols]).astype(BF16)

    finish(0, True)
    service_x(2)
    service_far(1)
    prefix_swap.wait_recv()
    finish(1, False)
    sq[...] = jnp.broadcast_to(jnp.sum(sq[...], axis=1, keepdims=True), (512, 128))

    def sqs(d):
        return remote(sq.at[y_quarter[d]], sq_recv.at[d], sq_s.at[d], sq_r.at[d], row(d))

    for d in range(1, Y):
        sqs(d).start()

    def rs(j, kind):
        src, dst, step = {
            0: (terms.at[j, 0, y_quarter[2]], ra_p.at[j], 1),
            1: (terms.at[j, 1, y_quarter[2]], ra_m.at[j], 3),
            2: (terms.at[j, 1, y_quarter[1]], rc_p.at[j], 1),
            3: (terms.at[j, 0, y_quarter[3]], rc_m.at[j], 3),
            4: (terms.at[j, 0, y_quarter[1]], rb_p.at[j], 1),
            5: (terms.at[j, 1, y_quarter[3]], rb_m.at[j], 3),
        }[kind]
        return remote(src, dst, rs_s.at[j, kind], rs_r.at[j, kind], row(step))

    def project(j):
        for place in range(4):
            wc(j, place).wait_recv()
        for side in range(2):
            weights = wt[j, pl.ds(2 * side, 2)].reshape(256, 1024)
            terms[j, side] = dot(hidden[...], weights, 1, 1).astype(BF16)
        for kind in range(4):
            rs(j, kind).start()

    def relay(j):
        for side, part, kind in ((0, ra_p, 0), (1, ra_m, 1)):
            rs(j, kind).wait_recv()
            rows = y_quarter[1 if side == 0 else 3]
            terms[j, side, rows] = (terms[j, side, rows].astype(F32) + part[j].astype(F32)).astype(BF16)
            rs(j, 4 + side).start()

    def final(j, scale):
        for kind in (2, 3, 4, 5):
            rs(j, kind).wait_recv()
        s = (j + 1) // 2
        zz = lax.rem(z + s * (1 - 2 * lax.rem(j, 2)) + Z, Z)
        for side, b, d in ((0, rb_p, rc_m), (1, rb_m, rc_p)):
            total = terms[j, side, y_quarter[0]].astype(F32) + b[j].astype(F32) + d[j].astype(F32)
            for n in range(2):
                xx = lax.rem(x + (0, 3, 1, 2)[2 * side + n], X)
                cols = pl.ds(pl.multiple_of((xx * Z + zz) * 128, 128), 128)
                out_ref[:, cols] = (total[:, n * 128:(n + 1) * 128] * scale).astype(BF16)

    def step(i, _):
        @pl.when(i < 5)
        def _():
            service_x(i + 3)

        @pl.when(i < 6)
        def _():
            service_far(i + 2)

        @pl.when(i < 8)
        def _():
            project(i)

        @pl.when((i >= 1) & (i < 9))
        def _():
            relay(i - 1)

        @pl.when(i == 1)
        def _():
            for d in range(1, Y):
                sqs(d).wait()
            total = sq[y_quarter[0]] + sq_recv[1] + sq_recv[2] + sq_recv[3]
            sq_recv[0] = lax.rsqrt(total / (Y * 1024) + EPS)

        @pl.when(i >= 2)
        def _():
            final(i - 2, sq_recv[0])

        return 0

    lax.fori_loop(0, 10, step, 0)

    for dst in range(1, Z):
        wz(max(dst - 2, 0), dst).wait_send()
    state_swap.wait_send()
    prefix_swap.wait_send()
    for d in range(1, Z):
        tz(d).wait_send()
        pz(d).wait_send()
    for d in range(1, X):
        lx(d).wait_send()

    def drain(j, _):
        for kind in range(4):
            wx(j, kind).wait_send()
            wc(j, kind).wait_send()
        for kind in range(6):
            rs(j, kind).wait_send()
        return 0

    lax.fori_loop(0, 8, drain, 0)


def shards(queries, key_input, value_input, gate_input, kv_state, norm_gain, out_weight):
    y = lax.axis_index("head")
    gain = lax.dynamic_slice_in_dim(norm_gain, y * 1024, 1024).reshape(1, 1024)
    hbm = pl.BlockSpec(memory_space=pl.ANY)
    vmem = pl.BlockSpec(memory_space=pltpu.VMEM)
    dma = pltpu.SemaphoreType.DMA
    scratch = [
        pltpu.VMEM((512, 1024), BF16), pltpu.VMEM((512, 1024), BF16), pltpu.VMEM((512, 1024), BF16),
        pltpu.VMEM((512, 1024), BF16), pltpu.VMEM((8, DH, DH), F32), pltpu.VMEM((1024, 64), BF16),
        pltpu.VMEM((Z, X, 2, 64, 1024), BF16),
        pltpu.VMEM((2, 4, DH, DH), F32), pltpu.VMEM((4, DH, DH), F32),
        pltpu.VMEM((Z, 64, DH), BF16), pltpu.VMEM((Z, 64, DH), BF16), pltpu.VMEM((Z, 64, DH), F32),
        pltpu.VMEM((64, DH), BF16), pltpu.VMEM((X, 64, DH), BF16),
        pltpu.VMEM((Z, 64, DH), BF16), pltpu.VMEM((Z, 64, DH), BF16),
        pltpu.VMEM((4, DH, DH), F32), pltpu.VMEM((4, DH, DH), F32),
        pltpu.VMEM((512, 1024), F32), pltpu.VMEM((512, 1024), F32), pltpu.VMEM((512, 1024), BF16),
        pltpu.VMEM((512, 128), F32), pltpu.VMEM((Y, 128, 128), F32),
        pltpu.VMEM((Z, 2, 512, 256), BF16),
    ] + [pltpu.VMEM((Z, 128, 256), BF16)] * 6 + [
        dma((6,)), dma((Z,)), dma((Z,)), dma((Z, 4)), dma((Z, 4)), dma((Z, 4)), dma((Z, 4)),
        dma, dma, dma((Z,)), dma((Z,)), dma((X,)), dma((X,)), dma((Z,)), dma((Z,)),
        dma, dma, dma((Y,)), dma((Y,)), dma((Z, 6)), dma((Z, 6)),
    ]
    return pl.pallas_call(
        body,
        out_shape=jax.ShapeDtypeStruct((128, 4096), BF16),
        in_specs=[hbm, hbm, hbm, hbm, hbm, vmem, hbm],
        out_specs=vmem,
        scratch_shapes=scratch,
        compiler_params=pltpu.CompilerParams(
            collective_id=0, has_side_effects=True, vmem_limit_bytes=48 << 20
        ),
        name="layer",
    )(queries, key_input, value_input, gate_input, kv_state, gain, out_weight)


def solution(mesh):
    in_specs = (
        P("seq", "head"),
        P("seq", "head"),
        P("seq", "head"),
        P("seq", "head"),
        P("head", None, None),
        P(),
        P("head", "seq"),
    )
    out_specs = P(("seq", "head"), None)
    return jax.shard_map(shards, mesh=mesh, in_specs=in_specs, out_specs=out_specs, check_vma=False)
```

```python
import jax
import jax.numpy as jnp
from jax import lax
from jax.experimental import pallas as pl
from jax.experimental.pallas import tpu as pltpu
from jax.sharding import PartitionSpec as P

MESH = pl.DeviceIdType.MESH
DH = 128
X, Z, Y = 4, 8, 4
SPLIT = 384
EPS = 1e-05
F32, BF16 = jnp.float32, jnp.bfloat16


def dot(a, b, ca, cb):
    return lax.dot_general(a, b, (((ca,), (cb,)), ((), ())), preferred_element_type=F32)


def body(
    q_hbm, k_hbm, v_hbm, g_hbm, kv_hbm, gain_hbm, w_hbm, out_ref,
    q, k, v, g, kv, gain, wt,
    s_own, s_other, t_send, t_recv, line, l_send, l_recv, p_send, p_chip, c_send, c_recv,
    inner, gated, hidden, sq, sq_recv, terms,
    ra_p, ra_m, rb_p, rb_m, rc_p, rc_m,
    load, wz_s, wz_r, wx_s, wx_r, wc_s, wc_r,
    sc_s, sc_r, tz_s, tz_r, lx_s, lx_r, pz_s, pz_r, cc_s, cc_r, sq_s, sq_r,
    rs_s, rs_r,
):
    seq, y = lax.axis_index("seq"), lax.axis_index("head")
    c = lax.rem(seq, 2)
    chip = seq // 2
    z = lax.rem(chip, Z)
    x = chip // Z

    def at(xx, zz, cc):
        return {"seq": (lax.rem(xx + X, X) * Z + lax.rem(zz + Z, Z)) * 2 + cc}

    def row(step):
        return {"head": lax.rem(y + step + Y, Y)}

    partner = at(x, z, 1 - c)
    y_quarter = [pl.ds(pl.multiple_of(lax.rem(y + d, Y) * 128, 128), 128) for d in range(Y)]

    own_gain = gain_hbm.at[:, pl.ds(pl.multiple_of(y * 1024, 1024), 1024)]
    loads = [(w_hbm, wt.at[0, 0, c]), (k_hbm, k), (v_hbm, v), (q_hbm, q), (kv_hbm, kv), (g_hbm, g), (own_gain, gain)]
    copies = [pltpu.make_async_copy(a, b, load.at[i]) for i, (a, b) in enumerate(loads)]
    for copy in copies:
        copy.start()
    barrier = pltpu.get_barrier_semaphore()
    partners = [partner] + [at(x, z + d, c) for d in range(1, Z)] + [at(x + d, z, c) for d in range(1, X)]
    partners += [row(d) for d in range(1, Y)]
    for device in partners:
        pl.semaphore_signal(barrier, inc=1, device_id=device, device_id_type=MESH)
    def remote(src, dst, ssem, rsem, device):
        return pltpu.make_async_remote_copy(
            src_ref=src, dst_ref=dst, send_sem=ssem, recv_sem=rsem, device_id=device, device_id_type=MESH
        )

    part = (slice(0, SPLIT), slice(SPLIT, 1024))

    def wz(place, dst, which):
        src = dst - 2 if dst > 2 else 0
        index = place if which == 0 else 4
        return remote(
            wt.at[src, place, c, :, part[which]], wt.at[dst, place, c, :, part[which]],
            wz_s.at[index, dst], wz_r.at[index, dst], at(x, z + (1 if dst % 2 else -1), c),
        )

    def wx(j, kind, which):
        rows = pl.ds(0, 64) if kind < 2 else pl.ds(32 * (kind - 2), 32)
        src, dst = (0, 1 + kind) if kind < 2 else (kind - 1, 3)
        index = 8 if which == 0 else j
        return remote(
            wt.at[j, src, c, rows, part[which]], wt.at[j, dst, c, rows, part[which]],
            wx_s.at[index, kind], wx_r.at[index, kind], at(x + (1 if kind % 2 == 0 else -1), z, c),
        )

    def wc(j):
        block = wt.at[j, :, c]
        return remote(block, block, wc_s.at[j], wc_r.at[j], partner)

    def spread(j):
        wx(j, 0, 1).start()
        wx(j, 1, 1).start()

    def start_weights():
        for dst in (1, 2):
            wz(0, dst, 1).start()
        for kind in (0, 1):
            wx(0, kind, 0).start()
        spread(0)
        for dst in (1, 2):
            wz(0, dst, 0).start()

    def ring_z(s, place, which):
        for dst in (2 * s - 1, 2 * s):
            if dst < 8:
                wz(place, dst, which).wait_recv()
                if dst < 6:
                    wz(place, dst + 2, which).start()

    def service_b(s):
        ring_z(s, 0, 1)
        for j in (2 * s - 1, 2 * s):
            if j < 8:
                spread(j)

    def service_a(s):
        for place in range(4):
            ring_z(s, place, 0)

    def near_a():
        for kind in (0, 1):
            wx(0, kind, 0).wait_recv()
            wx(0, kind + 2, 0).start()
        for dst in (1, 2):
            for place in (1, 2):
                wz(place, dst, 0).start()

    def far_a():
        for kind in (2, 3):
            wx(0, kind, 0).wait_recv()
        for dst in (1, 2):
            wz(3, dst, 0).start()

    def near(j):
        for kind in (0, 1):
            wx(j, kind, 1).wait_recv()
            wx(j, kind + 2, 1).start()

    def far(j):
        for kind in (2, 3):
            wx(j, kind, 1).wait_recv()
        wc(j).start()

    def states(which):
        for h in range(4):
            cols = pl.ds(pl.multiple_of((which * 4 + h) * DH, DH), DH)
            s_own[which, h] = dot(k[:, cols], v[:, cols], 0, 0)

    copies[1].wait()
    copies[2].wait()
    states(1 - c)
    pl.semaphore_wait(barrier, len(partners))
    state_swap = remote(s_own.at[1 - c], s_other, sc_s, sc_r, partner)
    state_swap.start()
    copies[0].wait()
    start_weights()
    states(c)

    copies[3].wait()
    lower = lax.broadcasted_iota(jnp.int32, (256, 256), 0) >= lax.broadcasted_iota(jnp.int32, (256, 256), 1)

    def local(h):
        cols = slice(h * DH, (h + 1) * DH)
        for r in range(2):
            rows = slice(r * 256, (r + 1) * 256)
            q_rows = q[rows, cols]
            near = jnp.where(lower, dot(q_rows, k[rows, cols], 1, 1), 0.0).astype(BF16)
            total = dot(near, v[rows, cols], 1, 0)
            if r == 1:
                far = dot(q_rows, k[0:256, cols], 1, 1).astype(BF16)
                total = total + dot(far, v[0:256, cols], 1, 0)
            inner[rows, cols] = total

    local(0)
    state_swap.wait_recv()
    for h in range(4):
        t = (s_own[c, h] + s_other[h]).astype(BF16)
        t_send[2 * h] = t[0:64]
        t_send[2 * h + 1] = t[64:128]

    def tz(d):
        to = lax.rem(z + d, Z)
        return remote(t_send.at[to], t_recv.at[z], tz_s.at[d], tz_r.at[d], at(x, z + d, c))

    def pz(d):
        to = lax.rem(z + d, Z)
        return remote(p_send.at[to], p_chip.at[z], pz_s.at[d], pz_r.at[d], at(x, z + d, c))

    def lx(d):
        return remote(l_send, l_recv.at[d], lx_s.at[d], lx_r.at[d], at(x + d, z, c))

    for d in (4, 3, 5, 2, 6, 1, 7):
        tz(d).start()
    t_recv[z] = t_send[z]
    local(1)
    local(2)
    service_b(1)
    local(3)
    for d in range(1, Z):
        tz(d).wait_recv()
    total = jnp.zeros((64, DH), F32)
    for i in range(Z):
        line[i] = total
        total = total + t_recv[i].astype(F32)
    l_send[...] = total.astype(BF16)
    for d in (2, 1, 3):
        lx(d).start()
    near_a()
    service_b(2)
    near(0)
    local(4)
    for d in range(1, X):
        lx(d).wait_recv()
    before = jnp.zeros((64, DH), F32)
    for d in range(1, X):
        before = before + jnp.where(x >= d, l_recv[d].astype(F32), 0.0)
    for i in range(Z):
        p_send[i] = (line[i] + before).astype(BF16)
    for d in (4, 3, 5, 2, 6, 1, 7):
        pz(d).start()
    p_chip[z] = p_send[z]
    far_a()
    far(0)
    service_b(3)
    local(5)
    local(6)
    local(7)
    near(1)
    copies[5].wait()
    copies[6].wait()
    for i in range(4):
        rows = slice(i * 128, (i + 1) * 128)
        gated[rows] = gain[...] * jax.nn.sigmoid(g[rows].astype(F32))
    near(2)
    copies[4].wait()
    for d in range(1, Z):
        pz(d).wait_recv()
    own_part = (1 - c).astype(F32)
    other_part = c.astype(F32)
    for h in range(4):
        base = jnp.concatenate([p_chip[2 * h].astype(F32), p_chip[2 * h + 1].astype(F32)], axis=0)
        c_send[h] = base + own_part * s_own[c, h]
        s_other[h] = base + other_part * s_other[h]
    prefix_swap = remote(c_send, c_recv, cc_s, cc_r, partner)
    prefix_swap.start()

    def carried(h, state):
        hi = state.astype(BF16)
        lo = (state - hi.astype(F32)).astype(BF16)
        return jnp.concatenate([hi, lo], axis=0)

    def finish(half, first):
        prefix = s_other if half == 0 else c_recv
        which = c if half == 0 else 1 - c
        for h in range(4):
            state = carried(h, kv[which * 4 + h] + prefix[h])
            cols = pl.ds(pl.multiple_of((which * 4 + h) * DH, DH), DH)
            qq = q[:, cols]
            attn = inner[:, cols] + dot(jnp.concatenate([qq, qq], axis=1), state, 1, 0)
            attn = attn.astype(BF16).astype(F32)
            square = attn * attn
            if first and h == 0:
                sq[...] = square
            else:
                sq[...] += square
            hidden[:, cols] = (attn * gated[:, cols]).astype(BF16)

    finish(0, True)
    service_b(4)
    service_a(1)
    far(1)
    prefix_swap.wait_recv()
    finish(1, False)
    sq[...] = jnp.broadcast_to(jnp.sum(sq[...], axis=1, keepdims=True), (512, 128))

    def sqs(d):
        return remote(sq.at[y_quarter[d]], sq_recv.at[d], sq_s.at[d], sq_r.at[d], row(d))

    for d in range(1, Y):
        sqs(d).start()

    def rs(j, kind):
        src, dst, step = {
            0: (terms.at[j, 0, y_quarter[2]], ra_p.at[j], 1),
            1: (terms.at[j, 1, y_quarter[2]], ra_m.at[j], 3),
            2: (terms.at[j, 1, y_quarter[1]], rc_p.at[j], 1),
            3: (terms.at[j, 0, y_quarter[3]], rc_m.at[j], 3),
            4: (terms.at[j, 0, y_quarter[1]], rb_p.at[j], 1),
            5: (terms.at[j, 1, y_quarter[3]], rb_m.at[j], 3),
        }[kind]
        return remote(src, dst, rs_s.at[j, kind], rs_r.at[j, kind], row(step))

    def project(j):
        wc(j).wait_recv()
        for side in range(2):
            weights = wt[j, pl.ds(2 * side, 2)].reshape(256, 1024)
            terms[j, side] = dot(hidden[...], weights, 1, 1).astype(BF16)
        for kind in range(4):
            rs(j, kind).start()

    def relay(j):
        for side, part, kind in ((0, ra_p, 0), (1, ra_m, 1)):
            rs(j, kind).wait_recv()
            rows = y_quarter[1 if side == 0 else 3]
            terms[j, side, rows] = (terms[j, side, rows].astype(F32) + part[j].astype(F32)).astype(BF16)
            rs(j, 4 + side).start()

    def final(j, scale):
        for kind in (2, 3, 4, 5):
            rs(j, kind).wait_recv()
        s = (j + 1) // 2
        zz = lax.rem(z + s * (1 - 2 * lax.rem(j, 2)) + Z, Z)
        for side, b, d in ((0, rb_p, rc_m), (1, rb_m, rc_p)):
            total = terms[j, side, y_quarter[0]].astype(F32) + b[j].astype(F32) + d[j].astype(F32)
            for n in range(2):
                xx = lax.rem(x + (0, 3, 1, 2)[2 * side + n], X)
                cols = pl.ds(pl.multiple_of((xx * Z + zz) * 128, 128), 128)
                out_ref[:, cols] = (total[:, n * 128:(n + 1) * 128] * scale).astype(BF16)

    def step(i, _):
        @pl.when(i == 0)
        def _():
            near(3)
            far(2)

        @pl.when(i == 1)
        def _():
            near(4)
            service_a(2)
            far(3)

        @pl.when(i == 2)
        def _():
            near(5)
            far(4)

        @pl.when(i == 3)
        def _():
            near(6)
            service_a(3)
            far(5)

        @pl.when(i == 4)
        def _():
            near(7)
            far(6)

        @pl.when(i == 5)
        def _():
            service_a(4)
            far(7)

        @pl.when(i < 8)
        def _():
            project(i)

        @pl.when((i >= 1) & (i < 9))
        def _():
            relay(i - 1)

        @pl.when(i == 1)
        def _():
            for d in range(1, Y):
                sqs(d).wait()
            total = sq[y_quarter[0]] + sq_recv[1] + sq_recv[2] + sq_recv[3]
            sq_recv[0] = lax.rsqrt(total / (Y * 1024) + EPS)

        @pl.when(i >= 2)
        def _():
            final(i - 2, sq_recv[0])

        return 0

    lax.fori_loop(0, 10, step, 0)

    for dst in range(1, Z):
        wz(0, dst, 1).wait_send()
        for place in range(4):
            wz(place, dst, 0).wait_send()
    for kind in range(4):
        wx(0, kind, 0).wait_send()
    state_swap.wait_send()
    prefix_swap.wait_send()
    for d in range(1, Z):
        tz(d).wait_send()
        pz(d).wait_send()
    for d in range(1, X):
        lx(d).wait_send()

    def drain(j, _):
        for kind in range(4):
            wx(j, kind, 1).wait_send()
        wc(j).wait_send()
        for kind in range(6):
            rs(j, kind).wait_send()
        return 0

    lax.fori_loop(0, 8, drain, 0)


def shards(queries, key_input, value_input, gate_input, kv_state, norm_gain, out_weight):
    hbm = pl.BlockSpec(memory_space=pltpu.HBM)
    vmem = pl.BlockSpec(memory_space=pltpu.VMEM)
    dma = pltpu.SemaphoreType.DMA
    scratch = [
        pltpu.VMEM((512, 1024), BF16), pltpu.VMEM((512, 1024), BF16), pltpu.VMEM((512, 1024), BF16),
        pltpu.VMEM((512, 1024), BF16), pltpu.VMEM((8, DH, DH), F32), pltpu.VMEM((1, 1024), F32),
        pltpu.VMEM((Z, X, 2, 64, 1024), BF16),
        pltpu.VMEM((2, 4, DH, DH), F32), pltpu.VMEM((4, DH, DH), F32),
        pltpu.VMEM((Z, 64, DH), BF16), pltpu.VMEM((Z, 64, DH), BF16), pltpu.VMEM((Z, 64, DH), F32),
        pltpu.VMEM((64, DH), BF16), pltpu.VMEM((X, 64, DH), BF16),
        pltpu.VMEM((Z, 64, DH), BF16), pltpu.VMEM((Z, 64, DH), BF16),
        pltpu.VMEM((4, DH, DH), F32), pltpu.VMEM((4, DH, DH), F32),
        pltpu.VMEM((512, 1024), F32), pltpu.VMEM((512, 1024), F32), pltpu.VMEM((512, 1024), BF16),
        pltpu.VMEM((512, 128), F32), pltpu.VMEM((Y, 128, 128), F32),
        pltpu.VMEM((Z, 2, 512, 256), BF16),
    ] + [pltpu.VMEM((Z, 128, 256), BF16)] * 6 + [
        dma((7,)), dma((5, Z)), dma((5, Z)), dma((Z + 1, 4)), dma((Z + 1, 4)), dma((Z,)), dma((Z,)),
        dma, dma, dma((Z,)), dma((Z,)), dma((X,)), dma((X,)), dma((Z,)), dma((Z,)),
        dma, dma, dma((Y,)), dma((Y,)), dma((Z, 6)), dma((Z, 6)),
    ]
    return pl.pallas_call(
        body,
        out_shape=jax.ShapeDtypeStruct((128, 4096), BF16),
        in_specs=[hbm] * 7,
        out_specs=vmem,
        scratch_shapes=scratch,
        compiler_params=pltpu.CompilerParams(
            collective_id=0, has_side_effects=True, vmem_limit_bytes=60 << 20
        ),
        name="layer",
    )(queries, key_input, value_input, gate_input, kv_state, norm_gain.reshape(1, 4096), out_weight.T)


def solution(mesh):
    in_specs = (
        P("seq", "head"),
        P("seq", "head"),
        P("seq", "head"),
        P("seq", "head"),
        P("head", None, None),
        P(),
        P("head", "seq"),
    )
    out_specs = P(("seq", "head"), None)
    return jax.shard_map(shards, mesh=mesh, in_specs=in_specs, out_specs=out_specs, check_vma=False)
```

```python
import jax
import jax.numpy as jnp
from jax import lax
from jax.experimental import pallas as pl
from jax.experimental.pallas import tpu as pltpu
from jax.sharding import PartitionSpec as P

MESH = pl.DeviceIdType.MESH
DH = 128
X, Z, Y = 4, 8, 4
SPLIT = 384
EPS = 1e-05
F32, BF16 = jnp.float32, jnp.bfloat16


def dot(a, b, ca, cb):
    return lax.dot_general(a, b, (((ca,), (cb,)), ((), ())), preferred_element_type=F32)


def body(
    q_hbm, k_hbm, v_hbm, g_hbm, kv_hbm, gain_hbm, w_hbm, out_ref,
    q, k, v, g, kv, gain, wt,
    s_own, s_other, t_send, t_recv, line, l_send, l_recv, p_send, p_chip, c_send, c_recv,
    inner, gated, hidden, squares, sq_send, sq_recv, scale, terms,
    ra_p, ra_m, rb_p, rb_m, rc_p, rc_m,
    load, wz_s, wz_r, wx_s, wx_r, wc_s, wc_r,
    sc_s, sc_r, tz_s, tz_r, lx_s, lx_r, pz_s, pz_r, cc_s, cc_r, sq_s, sq_r,
    rs_s, rs_r,
):
    seq, y = lax.axis_index("seq"), lax.axis_index("head")
    c = lax.rem(seq, 2)
    chip = seq // 2
    z = lax.rem(chip, Z)
    x = chip // Z

    def at(xx, zz, cc):
        return {"seq": (lax.rem(xx + X, X) * Z + lax.rem(zz + Z, Z)) * 2 + cc}

    def row(step):
        return {"head": lax.rem(y + step + Y, Y)}

    partner = at(x, z, 1 - c)
    y_quarter = [pl.ds(pl.multiple_of(lax.rem(y + d, Y) * 128, 128), 128) for d in range(Y)]

    own_gain = gain_hbm.at[:, pl.ds(pl.multiple_of(y * 1024, 1024), 1024)]
    loads = [(w_hbm, wt.at[0, 0, c]), (k_hbm, k), (v_hbm, v), (q_hbm, q), (kv_hbm, kv), (g_hbm, g), (own_gain, gain)]
    copies = [pltpu.make_async_copy(a, b, load.at[i]) for i, (a, b) in enumerate(loads)]
    for copy in copies:
        copy.start()
    barrier = pltpu.get_barrier_semaphore()
    partners = [partner] + [at(x, z + d, c) for d in range(1, Z)] + [at(x + d, z, c) for d in range(1, X)]
    partners += [row(d) for d in range(1, Y)]
    for device in partners:
        pl.semaphore_signal(barrier, inc=1, device_id=device, device_id_type=MESH)
    def remote(src, dst, ssem, rsem, device):
        return pltpu.make_async_remote_copy(
            src_ref=src, dst_ref=dst, send_sem=ssem, recv_sem=rsem, device_id=device, device_id_type=MESH
        )

    part = (slice(0, SPLIT), slice(SPLIT, 1024))

    def wz(place, dst, which):
        src = dst - 2 if dst > 2 else 0
        index = place if which == 0 else 4
        return remote(
            wt.at[src, place, c, :, part[which]], wt.at[dst, place, c, :, part[which]],
            wz_s.at[index, dst], wz_r.at[index, dst], at(x, z + (1 if dst % 2 else -1), c),
        )

    def wx(j, kind, which):
        rows = pl.ds(0, 64) if kind < 2 else pl.ds(32 * (kind - 2), 32)
        src, dst = (0, 1 + kind) if kind < 2 else (kind - 1, 3)
        index = 8 if which == 0 else j
        return remote(
            wt.at[j, src, c, rows, part[which]], wt.at[j, dst, c, rows, part[which]],
            wx_s.at[index, kind], wx_r.at[index, kind], at(x + (1 if kind % 2 == 0 else -1), z, c),
        )

    def wc(j):
        block = wt.at[j, :, c]
        return remote(block, block, wc_s.at[j], wc_r.at[j], partner)

    def spread(j):
        wx(j, 0, 1).start()
        wx(j, 1, 1).start()

    def start_weights():
        for dst in (1, 2):
            wz(0, dst, 1).start()
        for kind in (0, 1):
            wx(0, kind, 0).start()
        spread(0)
        for dst in (1, 2):
            wz(0, dst, 0).start()

    def ring_z(s, place, which):
        for dst in (2 * s - 1, 2 * s):
            if dst < 8:
                wz(place, dst, which).wait_recv()
                if dst < 6:
                    wz(place, dst + 2, which).start()

    def service_b(s):
        ring_z(s, 0, 1)
        for j in (2 * s - 1, 2 * s):
            if j < 8:
                spread(j)

    def service_a(s):
        for place in range(4):
            ring_z(s, place, 0)

    def near_a():
        for kind in (0, 1):
            wx(0, kind, 0).wait_recv()
            wx(0, kind + 2, 0).start()
        for dst in (1, 2):
            for place in (1, 2):
                wz(place, dst, 0).start()

    def far_a():
        for kind in (2, 3):
            wx(0, kind, 0).wait_recv()
        for dst in (1, 2):
            wz(3, dst, 0).start()

    def near(j):
        for kind in (0, 1):
            wx(j, kind, 1).wait_recv()
            wx(j, kind + 2, 1).start()

    def far(j):
        for kind in (2, 3):
            wx(j, kind, 1).wait_recv()
        wc(j).start()

    def states(which):
        for h in range(4):
            cols = pl.ds(pl.multiple_of((which * 4 + h) * DH, DH), DH)
            s_own[which, h] = dot(k[:, cols], v[:, cols], 0, 0)

    copies[1].wait()
    copies[2].wait()
    states(1 - c)
    pl.semaphore_wait(barrier, len(partners))
    state_swap = remote(s_own.at[1 - c], s_other, sc_s, sc_r, partner)
    state_swap.start()
    copies[0].wait()
    start_weights()
    states(c)

    copies[3].wait()
    lower = lax.broadcasted_iota(jnp.int32, (256, 256), 0) >= lax.broadcasted_iota(jnp.int32, (256, 256), 1)

    def local(h):
        cols = slice(h * DH, (h + 1) * DH)
        for r in range(2):
            rows = slice(r * 256, (r + 1) * 256)
            q_rows = q[rows, cols]
            near = jnp.where(lower, dot(q_rows, k[rows, cols], 1, 1), 0.0).astype(BF16)
            total = dot(near, v[rows, cols], 1, 0)
            if r == 1:
                far = dot(q_rows, k[0:256, cols], 1, 1).astype(BF16)
                total = total + dot(far, v[0:256, cols], 1, 0)
            inner[rows, cols] = total

    local(0)
    state_swap.wait_recv()
    for h in range(4):
        t = (s_own[c, h] + s_other[h]).astype(BF16)
        t_send[2 * h] = t[0:64]
        t_send[2 * h + 1] = t[64:128]

    def tz(d):
        to = lax.rem(z + d, Z)
        return remote(t_send.at[to], t_recv.at[z], tz_s.at[d], tz_r.at[d], at(x, z + d, c))

    def pz(d):
        to = lax.rem(z + d, Z)
        return remote(p_send.at[to], p_chip.at[z], pz_s.at[d], pz_r.at[d], at(x, z + d, c))

    def lx(d):
        return remote(l_send, l_recv.at[d], lx_s.at[d], lx_r.at[d], at(x + d, z, c))

    for d in (4, 3, 5, 2, 6, 1, 7):
        tz(d).start()
    t_recv[z] = t_send[z]
    local(1)
    service_b(1)
    near_a()
    local(2)
    local(3)
    for d in range(1, Z):
        tz(d).wait_recv()
    total = jnp.zeros((64, DH), F32)
    for i in range(Z):
        line[i] = total
        total = total + t_recv[i].astype(F32)
    l_send[...] = total.astype(BF16)
    for d in (2, 1, 3):
        lx(d).start()
    service_b(2)
    far_a()
    near(0)
    local(4)
    for d in range(1, X):
        lx(d).wait_recv()
    before = jnp.zeros((64, DH), F32)
    for d in range(1, X):
        before = before + jnp.where(x >= d, l_recv[d].astype(F32), 0.0)
    for i in range(Z):
        p_send[i] = (line[i] + before).astype(BF16)
    for d in (4, 3, 5, 2, 6, 1, 7):
        pz(d).start()
    p_chip[z] = p_send[z]
    near(1)
    near(2)
    service_b(3)
    local(5)
    local(6)
    local(7)
    service_a(1)
    copies[5].wait()
    copies[6].wait()
    for i in range(4):
        rows = slice(i * 128, (i + 1) * 128)
        gated[rows] = gain[...] * jax.nn.sigmoid(g[rows].astype(F32))
    copies[4].wait()
    for d in range(1, Z):
        pz(d).wait_recv()
    own_part = (1 - c).astype(F32)
    other_part = c.astype(F32)
    for h in range(4):
        base = jnp.concatenate([p_chip[2 * h].astype(F32), p_chip[2 * h + 1].astype(F32)], axis=0)
        c_send[h] = base + own_part * s_own[c, h]
        s_other[h] = base + other_part * s_other[h]
    prefix_swap = remote(c_send, c_recv, cc_s, cc_r, partner)
    prefix_swap.start()

    def carried(h, state):
        hi = state.astype(BF16)
        lo = (state - hi.astype(F32)).astype(BF16)
        return jnp.concatenate([hi, lo], axis=0)

    def finish(half, first):
        prefix = s_other if half == 0 else c_recv
        which = c if half == 0 else 1 - c
        for h in range(4):
            state = carried(h, kv[which * 4 + h] + prefix[h])
            cols = pl.ds(pl.multiple_of((which * 4 + h) * DH, DH), DH)
            qq = q[:, cols]
            attn = inner[:, cols] + dot(jnp.concatenate([qq, qq], axis=1), state, 1, 0)
            attn = attn.astype(BF16).astype(F32)
            square = attn * attn
            if first and h == 0:
                squares[...] = square
            else:
                squares[...] += square
            hidden[:, cols] = (attn * gated[:, cols]).astype(BF16)

    finish(0, True)
    near(3)
    near(4)
    service_b(4)
    far(0)
    far(1)
    prefix_swap.wait_recv()
    finish(1, False)
    for d in range(Y):
        sums = jnp.sum(jnp.transpose(squares[y_quarter[d]]), axis=0, keepdims=True)
        sq_send[d] = jnp.broadcast_to(sums, (8, 128))

    def sqs(d):
        return remote(sq_send.at[d], sq_recv.at[d], sq_s.at[d], sq_r.at[d], row(d))

    for d in range(1, Y):
        sqs(d).start()

    def rs(j, kind):
        src, dst, step = {
            0: (terms.at[j, 0, y_quarter[2]], ra_p.at[j], 1),
            1: (terms.at[j, 1, y_quarter[2]], ra_m.at[j], 3),
            2: (terms.at[j, 1, y_quarter[1]], rc_p.at[j], 1),
            3: (terms.at[j, 0, y_quarter[3]], rc_m.at[j], 3),
            4: (terms.at[j, 0, y_quarter[1]], rb_p.at[j], 1),
            5: (terms.at[j, 1, y_quarter[3]], rb_m.at[j], 3),
        }[kind]
        return remote(src, dst, rs_s.at[j, kind], rs_r.at[j, kind], row(step))

    def project(j):
        wc(j).wait_recv()
        for side in range(2):
            weights = wt[j, pl.ds(2 * side, 2)].reshape(256, 1024)
            terms[j, side] = dot(hidden[...], weights, 1, 1).astype(BF16)
            rs(j, side).start()

    def direct(j):
        rs(j, 2).start()
        rs(j, 3).start()

    def relay(j):
        for side, part, rows in ((0, ra_p, y_quarter[1]), (1, ra_m, y_quarter[3])):
            rs(j, side).wait_recv()
            terms[j, side, rows] = (terms[j, side, rows].astype(F32) + part[j].astype(F32)).astype(BF16)
            rs(j, 4 + side).start()

    def final(j):
        for kind in (2, 3, 4, 5):
            rs(j, kind).wait_recv()
        s = (j + 1) // 2
        zz = lax.rem(z + s * (1 - 2 * (j % 2)) + Z, Z)
        for side, b, d in ((0, rb_p, rc_m), (1, rb_m, rc_p)):
            total = terms[j, side, y_quarter[0]].astype(F32) + b[j].astype(F32) + d[j].astype(F32)
            for n in range(2):
                xx = lax.rem(x + (0, 3, 1, 2)[2 * side + n], X)
                cols = pl.ds(pl.multiple_of((xx * Z + zz) * 128, 128), 128)
                out_ref[:, cols] = (total[:, n * 128:(n + 1) * 128] * scale[...]).astype(BF16)

    project(0)
    direct(0)
    near(5)
    near(6)
    far(2)
    project(1)
    near(7)
    service_a(2)
    far(3)
    relay(0)
    project(2)
    direct(1)
    far(4)
    service_a(3)
    far(5)
    far(6)
    relay(1)
    project(3)
    direct(2)
    service_a(4)
    far(7)
    for d in range(1, Y):
        sqs(d).wait()
    total = sq_send[0] + sq_recv[1] + sq_recv[2] + sq_recv[3]
    factor = lax.rsqrt(total / (Y * 1024) + EPS)
    scale[...] = jnp.transpose(jnp.broadcast_to(factor[0:1], (128, 128)))
    relay(2)
    project(4)
    direct(3)
    final(0)
    relay(3)
    project(5)
    direct(4)
    final(1)
    relay(4)
    project(6)
    direct(5)
    final(2)
    relay(5)
    project(7)
    direct(6)
    final(3)
    relay(6)
    direct(7)
    final(4)
    relay(7)
    final(5)
    final(6)
    final(7)

    for dst in range(1, Z):
        wz(0, dst, 1).wait_send()
        for place in range(4):
            wz(place, dst, 0).wait_send()
    for kind in range(4):
        wx(0, kind, 0).wait_send()
    state_swap.wait_send()
    prefix_swap.wait_send()
    for d in range(1, Z):
        tz(d).wait_send()
        pz(d).wait_send()
    for d in range(1, X):
        lx(d).wait_send()

    def drain(j, _):
        for kind in range(4):
            wx(j, kind, 1).wait_send()
        wc(j).wait_send()
        for kind in range(6):
            rs(j, kind).wait_send()
        return 0

    lax.fori_loop(0, 8, drain, 0)


def shards(queries, key_input, value_input, gate_input, kv_state, norm_gain, out_weight):
    hbm = pl.BlockSpec(memory_space=pltpu.HBM)
    vmem = pl.BlockSpec(memory_space=pltpu.VMEM)
    dma = pltpu.SemaphoreType.DMA
    scratch = [
        pltpu.VMEM((512, 1024), BF16), pltpu.VMEM((512, 1024), BF16), pltpu.VMEM((512, 1024), BF16),
        pltpu.VMEM((512, 1024), BF16), pltpu.VMEM((8, DH, DH), F32), pltpu.VMEM((1, 1024), F32),
        pltpu.VMEM((Z, X, 2, 64, 1024), BF16),
        pltpu.VMEM((2, 4, DH, DH), F32), pltpu.VMEM((4, DH, DH), F32),
        pltpu.VMEM((Z, 64, DH), BF16), pltpu.VMEM((Z, 64, DH), BF16), pltpu.VMEM((Z, 64, DH), F32),
        pltpu.VMEM((64, DH), BF16), pltpu.VMEM((X, 64, DH), BF16),
        pltpu.VMEM((Z, 64, DH), BF16), pltpu.VMEM((Z, 64, DH), BF16),
        pltpu.VMEM((4, DH, DH), F32), pltpu.VMEM((4, DH, DH), F32),
        pltpu.VMEM((512, 1024), F32), pltpu.VMEM((512, 1024), F32), pltpu.VMEM((512, 1024), BF16),
        pltpu.VMEM((512, 128), F32), pltpu.VMEM((Y, 8, 128), F32), pltpu.VMEM((Y, 8, 128), F32),
        pltpu.VMEM((128, 128), F32),
        pltpu.VMEM((Z, 2, 512, 256), BF16),
    ] + [pltpu.VMEM((Z, 128, 256), BF16)] * 6 + [
        dma((7,)), dma((5, Z)), dma((5, Z)), dma((Z + 1, 4)), dma((Z + 1, 4)), dma((Z,)), dma((Z,)),
        dma, dma, dma((Z,)), dma((Z,)), dma((X,)), dma((X,)), dma((Z,)), dma((Z,)),
        dma, dma, dma((Y,)), dma((Y,)), dma((Z, 6)), dma((Z, 6)),
    ]
    return pl.pallas_call(
        body,
        out_shape=jax.ShapeDtypeStruct((128, 4096), BF16),
        in_specs=[hbm] * 7,
        out_specs=vmem,
        scratch_shapes=scratch,
        compiler_params=pltpu.CompilerParams(
            collective_id=0, has_side_effects=True, vmem_limit_bytes=60 << 20
        ),
        name="layer",
    )(queries, key_input, value_input, gate_input, kv_state, norm_gain.reshape(1, 4096), out_weight.T)


def solution(mesh):
    in_specs = (
        P("seq", "head"),
        P("seq", "head"),
        P("seq", "head"),
        P("seq", "head"),
        P("head", None, None),
        P(),
        P("head", "seq"),
    )
    out_specs = P(("seq", "head"), None)
    return jax.shard_map(shards, mesh=mesh, in_specs=in_specs, out_specs=out_specs, check_vma=False)
```

```python
import jax
import jax.numpy as jnp
from jax import lax
from jax.experimental import pallas as pl
from jax.experimental.pallas import tpu as pltpu
from jax.sharding import PartitionSpec as P

MESH = pl.DeviceIdType.MESH
DH = 128
X, Z, Y = 4, 8, 4
SPLIT = 384
EPS = 1e-05
F32, BF16 = jnp.float32, jnp.bfloat16


def dot(a, b, ca, cb):
    return lax.dot_general(a, b, (((ca,), (cb,)), ((), ())), preferred_element_type=F32)


def body(
    q_hbm, k_hbm, v_hbm, g_hbm, kv_hbm, gain_hbm, w_hbm, out_hbm,
    out_ref, q, k, v, g, kv, gain, wt,
    s_own, s_other, t_send, t_recv, line, l_send, l_recv, p_send, p_chip, c_send, c_recv,
    inner, gated, hidden, squares, sq_send, sq_recv, scale, terms,
    ra_p, ra_m, rb_p, rb_m, rc_p, rc_m,
    load, wz_s, wz_r, wx_s, wx_r, wc_s, wc_r,
    sc_s, sc_r, tz_s, tz_r, lx_s, lx_r, pz_s, pz_r, cc_s, cc_r, sq_s, sq_r,
    rs_s, rs_r, put_s,
):
    seq, y = lax.axis_index("seq"), lax.axis_index("head")
    c = lax.rem(seq, 2)
    chip = seq // 2
    z = lax.rem(chip, Z)
    x = chip // Z

    def at(xx, zz, cc):
        return {"seq": (lax.rem(xx + X, X) * Z + lax.rem(zz + Z, Z)) * 2 + cc}

    def row(step):
        return {"head": lax.rem(y + step + Y, Y)}

    partner = at(x, z, 1 - c)
    y_quarter = [pl.ds(pl.multiple_of(lax.rem(y + d, Y) * 128, 128), 128) for d in range(Y)]

    own_gain = gain_hbm.at[:, pl.ds(pl.multiple_of(y * 1024, 1024), 1024)]
    loads = [(w_hbm, wt.at[0, 0, c]), (k_hbm, k), (v_hbm, v), (q_hbm, q), (kv_hbm, kv), (g_hbm, g), (own_gain, gain)]
    copies = [pltpu.make_async_copy(a, b, load.at[i]) for i, (a, b) in enumerate(loads)]
    for copy in copies:
        copy.start()
    barrier = pltpu.get_barrier_semaphore()
    partners = [partner] + [at(x, z + d, c) for d in range(1, Z)] + [at(x + d, z, c) for d in range(1, X)]
    partners += [row(d) for d in range(1, Y)]
    for device in partners:
        pl.semaphore_signal(barrier, inc=1, device_id=device, device_id_type=MESH)
    def remote(src, dst, ssem, rsem, device):
        return pltpu.make_async_remote_copy(
            src_ref=src, dst_ref=dst, send_sem=ssem, recv_sem=rsem, device_id=device, device_id_type=MESH
        )

    part = (slice(0, SPLIT), slice(SPLIT, 1024))

    def wz(place, dst, which):
        src = dst - 2 if dst > 2 else 0
        index = place if which == 0 else 4
        return remote(
            wt.at[src, place, c, :, part[which]], wt.at[dst, place, c, :, part[which]],
            wz_s.at[index, dst], wz_r.at[index, dst], at(x, z + (1 if dst % 2 else -1), c),
        )

    def wx(j, kind, which):
        rows = pl.ds(0, 64) if kind < 2 else pl.ds(32 * (kind - 2), 32)
        src, dst = (0, 1 + kind) if kind < 2 else (kind - 1, 3)
        index = 8 if which == 0 else j
        return remote(
            wt.at[j, src, c, rows, part[which]], wt.at[j, dst, c, rows, part[which]],
            wx_s.at[index, kind], wx_r.at[index, kind], at(x + (1 if kind % 2 == 0 else -1), z, c),
        )

    def wc(j):
        block = wt.at[j, :, c]
        return remote(block, block, wc_s.at[j], wc_r.at[j], partner)

    def spread(j):
        wx(j, 0, 1).start()
        wx(j, 1, 1).start()

    def start_weights():
        for dst in (1, 2):
            wz(0, dst, 1).start()
        for kind in (0, 1):
            wx(0, kind, 0).start()
        spread(0)
        for dst in (1, 2):
            wz(0, dst, 0).start()

    def ring_z(s, place, which):
        for dst in (2 * s - 1, 2 * s):
            if dst < 8:
                wz(place, dst, which).wait_recv()
                if dst < 6:
                    wz(place, dst + 2, which).start()

    def service_b(s):
        ring_z(s, 0, 1)
        for j in (2 * s - 1, 2 * s):
            if j < 8:
                spread(j)

    def service_a(s):
        for place in range(4):
            ring_z(s, place, 0)

    def near_a():
        for kind in (0, 1):
            wx(0, kind, 0).wait_recv()
            wx(0, kind + 2, 0).start()
        for dst in (1, 2):
            for place in (1, 2):
                wz(place, dst, 0).start()

    def far_a():
        for kind in (2, 3):
            wx(0, kind, 0).wait_recv()
        for dst in (1, 2):
            wz(3, dst, 0).start()

    def near(j):
        for kind in (0, 1):
            wx(j, kind, 1).wait_recv()
            wx(j, kind + 2, 1).start()

    def far(j):
        for kind in (2, 3):
            wx(j, kind, 1).wait_recv()
        wc(j).start()

    def states(which):
        for h in range(4):
            cols = pl.ds(pl.multiple_of((which * 4 + h) * DH, DH), DH)
            s_own[which, h] = dot(k[:, cols], v[:, cols], 0, 0)

    copies[1].wait()
    copies[2].wait()
    states(1 - c)
    pl.semaphore_wait(barrier, len(partners))
    state_swap = remote(s_own.at[1 - c], s_other, sc_s, sc_r, partner)
    state_swap.start()
    copies[0].wait()
    start_weights()
    states(c)

    copies[3].wait()
    lower = lax.broadcasted_iota(jnp.int32, (256, 256), 0) >= lax.broadcasted_iota(jnp.int32, (256, 256), 1)

    def local(h):
        cols = slice(h * DH, (h + 1) * DH)
        for r in range(2):
            rows = slice(r * 256, (r + 1) * 256)
            q_rows = q[rows, cols]
            near = jnp.where(lower, dot(q_rows, k[rows, cols], 1, 1), 0.0).astype(BF16)
            total = dot(near, v[rows, cols], 1, 0)
            if r == 1:
                far = dot(q_rows, k[0:256, cols], 1, 1).astype(BF16)
                total = total + dot(far, v[0:256, cols], 1, 0)
            inner[rows, cols] = total

    local(0)
    state_swap.wait_recv()
    for h in range(4):
        t = (s_own[c, h] + s_other[h]).astype(BF16)
        t_send[2 * h] = t[0:64]
        t_send[2 * h + 1] = t[64:128]

    def tz(d):
        to = lax.rem(z + d, Z)
        return remote(t_send.at[to], t_recv.at[z], tz_s.at[d], tz_r.at[d], at(x, z + d, c))

    def pz(d):
        to = lax.rem(z + d, Z)
        return remote(p_send.at[to], p_chip.at[z], pz_s.at[d], pz_r.at[d], at(x, z + d, c))

    def lx(d):
        return remote(l_send, l_recv.at[d], lx_s.at[d], lx_r.at[d], at(x + d, z, c))

    for d in (4, 3, 5, 2, 6, 1, 7):
        tz(d).start()
    t_recv[z] = t_send[z]
    local(1)
    service_b(1)
    near_a()
    local(2)
    local(3)
    for d in range(1, Z):
        tz(d).wait_recv()
    total = jnp.zeros((64, DH), F32)
    for i in range(Z):
        line[i] = total
        total = total + t_recv[i].astype(F32)
    l_send[...] = total.astype(BF16)
    for d in (2, 1, 3):
        lx(d).start()
    service_b(2)
    far_a()
    near(0)
    local(4)
    for d in range(1, X):
        lx(d).wait_recv()
    before = jnp.zeros((64, DH), F32)
    for d in range(1, X):
        before = before + jnp.where(x >= d, l_recv[d].astype(F32), 0.0)
    for i in range(Z):
        p_send[i] = (line[i] + before).astype(BF16)
    for d in (4, 3, 5, 2, 6, 1, 7):
        pz(d).start()
    p_chip[z] = p_send[z]
    near(1)
    near(2)
    service_b(3)
    local(5)
    local(6)
    local(7)
    service_a(1)
    copies[5].wait()
    copies[6].wait()
    for i in range(4):
        rows = slice(i * 128, (i + 1) * 128)
        gated[rows] = gain[...] * jax.nn.sigmoid(g[rows].astype(F32))
    copies[4].wait()
    for d in range(1, Z):
        pz(d).wait_recv()
    own_part = (1 - c).astype(F32)
    other_part = c.astype(F32)
    for h in range(4):
        base = jnp.concatenate([p_chip[2 * h].astype(F32), p_chip[2 * h + 1].astype(F32)], axis=0)
        c_send[h] = base + own_part * s_own[c, h]
        s_other[h] = base + other_part * s_other[h]
    prefix_swap = remote(c_send, c_recv, cc_s, cc_r, partner)
    prefix_swap.start()

    def carried(h, state):
        hi = state.astype(BF16)
        lo = (state - hi.astype(F32)).astype(BF16)
        return jnp.concatenate([hi, lo], axis=0)

    def finish(half, first):
        prefix = s_other if half == 0 else c_recv
        which = c if half == 0 else 1 - c
        for h in range(4):
            state = carried(h, kv[which * 4 + h] + prefix[h])
            cols = pl.ds(pl.multiple_of((which * 4 + h) * DH, DH), DH)
            qq = q[:, cols]
            attn = inner[:, cols] + dot(jnp.concatenate([qq, qq], axis=1), state, 1, 0)
            attn = attn.astype(BF16).astype(F32)
            square = attn * attn
            if first and h == 0:
                squares[...] = square
            else:
                squares[...] += square
            hidden[:, cols] = (attn * gated[:, cols]).astype(BF16)

    finish(0, True)
    near(3)
    near(4)
    service_b(4)
    far(0)
    far(1)
    prefix_swap.wait_recv()
    finish(1, False)
    for d in range(Y):
        sums = jnp.sum(jnp.transpose(squares[y_quarter[d]]), axis=0, keepdims=True)
        sq_send[d] = jnp.broadcast_to(sums, (8, 128))

    def sqs(d):
        return remote(sq_send.at[d], sq_recv.at[d], sq_s.at[d], sq_r.at[d], row(d))

    for d in range(1, Y):
        sqs(d).start()

    def rs(j, kind):
        src, dst, step = {
            0: (terms.at[j, 0, y_quarter[2]], ra_p.at[j], 1),
            1: (terms.at[j, 1, y_quarter[2]], ra_m.at[j], 3),
            2: (terms.at[j, 1, y_quarter[1]], rc_p.at[j], 1),
            3: (terms.at[j, 0, y_quarter[3]], rc_m.at[j], 3),
            4: (terms.at[j, 0, y_quarter[1]], rb_p.at[j], 1),
            5: (terms.at[j, 1, y_quarter[3]], rb_m.at[j], 3),
        }[kind]
        return remote(src, dst, rs_s.at[j, kind], rs_r.at[j, kind], row(step))

    def project(j):
        wc(j).wait_recv()
        for side in range(2):
            weights = wt[j, pl.ds(2 * side, 2)].reshape(256, 1024)
            terms[j, side] = dot(hidden[...], weights, 1, 1).astype(BF16)
            rs(j, side).start()

    def direct(j):
        rs(j, 2).start()
        rs(j, 3).start()

    def relay(j):
        for side, part, rows in ((0, ra_p, y_quarter[1]), (1, ra_m, y_quarter[3])):
            rs(j, side).wait_recv()
            terms[j, side, rows] = (terms[j, side, rows].astype(F32) + part[j].astype(F32)).astype(BF16)
            rs(j, 4 + side).start()

    def put(j, place):
        s = (j + 1) // 2
        zz = lax.rem(z + s * (1 - 2 * (j % 2)) + Z, Z)
        xx = lax.rem(x + (0, 3, 1, 2)[place], X)
        cols = pl.ds(pl.multiple_of((xx * Z + zz) * 128, 128), 128)
        return pltpu.make_async_copy(out_ref.at[:, cols], out_hbm.at[:, cols], put_s.at[j, place])

    def final(j):
        for kind in (2, 3, 4, 5):
            rs(j, kind).wait_recv()
        s = (j + 1) // 2
        zz = lax.rem(z + s * (1 - 2 * (j % 2)) + Z, Z)
        for side, b, d in ((0, rb_p, rc_m), (1, rb_m, rc_p)):
            total = terms[j, side, y_quarter[0]].astype(F32) + b[j].astype(F32) + d[j].astype(F32)
            for n in range(2):
                xx = lax.rem(x + (0, 3, 1, 2)[2 * side + n], X)
                cols = pl.ds(pl.multiple_of((xx * Z + zz) * 128, 128), 128)
                out_ref[:, cols] = (total[:, n * 128:(n + 1) * 128] * scale[...]).astype(BF16)
                put(j, 2 * side + n).start()

    project(0)
    direct(0)
    near(5)
    near(6)
    far(2)
    project(1)
    near(7)
    service_a(2)
    far(3)
    relay(0)
    project(2)
    direct(1)
    far(4)
    service_a(3)
    far(5)
    far(6)
    relay(1)
    project(3)
    direct(2)
    service_a(4)
    far(7)
    for d in range(1, Y):
        sqs(d).wait()
    total = sq_send[0] + sq_recv[1] + sq_recv[2] + sq_recv[3]
    factor = lax.rsqrt(total / (Y * 1024) + EPS)
    scale[...] = jnp.transpose(jnp.broadcast_to(factor[0:1], (128, 128)))
    relay(2)
    project(4)
    direct(3)
    final(0)
    relay(3)
    project(5)
    direct(4)
    final(1)
    relay(4)
    project(6)
    direct(5)
    final(2)
    relay(5)
    project(7)
    direct(6)
    final(3)
    relay(6)
    direct(7)
    final(4)
    relay(7)
    final(5)
    final(6)
    final(7)

    for dst in range(1, Z):
        wz(0, dst, 1).wait_send()
        for place in range(4):
            wz(place, dst, 0).wait_send()
    for kind in range(4):
        wx(0, kind, 0).wait_send()
    for j in range(8):
        for place in range(4):
            put(j, place).wait()
    state_swap.wait_send()
    prefix_swap.wait_send()
    for d in range(1, Z):
        tz(d).wait_send()
        pz(d).wait_send()
    for d in range(1, X):
        lx(d).wait_send()

    def drain(j, _):
        for kind in range(4):
            wx(j, kind, 1).wait_send()
        wc(j).wait_send()
        for kind in range(6):
            rs(j, kind).wait_send()
        return 0

    lax.fori_loop(0, 8, drain, 0)


def shards(queries, key_input, value_input, gate_input, kv_state, norm_gain, out_weight):
    hbm = pl.BlockSpec(memory_space=pltpu.HBM)
    dma = pltpu.SemaphoreType.DMA
    scratch = [
        pltpu.VMEM((128, 4096), BF16),
        pltpu.VMEM((512, 1024), BF16), pltpu.VMEM((512, 1024), BF16), pltpu.VMEM((512, 1024), BF16),
        pltpu.VMEM((512, 1024), BF16), pltpu.VMEM((8, DH, DH), F32), pltpu.VMEM((1, 1024), F32),
        pltpu.VMEM((Z, X, 2, 64, 1024), BF16),
        pltpu.VMEM((2, 4, DH, DH), F32), pltpu.VMEM((4, DH, DH), F32),
        pltpu.VMEM((Z, 64, DH), BF16), pltpu.VMEM((Z, 64, DH), BF16), pltpu.VMEM((Z, 64, DH), F32),
        pltpu.VMEM((64, DH), BF16), pltpu.VMEM((X, 64, DH), BF16),
        pltpu.VMEM((Z, 64, DH), BF16), pltpu.VMEM((Z, 64, DH), BF16),
        pltpu.VMEM((4, DH, DH), F32), pltpu.VMEM((4, DH, DH), F32),
        pltpu.VMEM((512, 1024), F32), pltpu.VMEM((512, 1024), F32), pltpu.VMEM((512, 1024), BF16),
        pltpu.VMEM((512, 128), F32), pltpu.VMEM((Y, 8, 128), F32), pltpu.VMEM((Y, 8, 128), F32),
        pltpu.VMEM((128, 128), F32),
        pltpu.VMEM((Z, 2, 512, 256), BF16),
    ] + [pltpu.VMEM((Z, 128, 256), BF16)] * 6 + [
        dma((7,)), dma((5, Z)), dma((5, Z)), dma((Z + 1, 4)), dma((Z + 1, 4)), dma((Z,)), dma((Z,)),
        dma, dma, dma((Z,)), dma((Z,)), dma((X,)), dma((X,)), dma((Z,)), dma((Z,)),
        dma, dma, dma((Y,)), dma((Y,)), dma((Z, 6)), dma((Z, 6)),
        dma((8, 4)),
    ]
    return pl.pallas_call(
        body,
        out_shape=jax.ShapeDtypeStruct((128, 4096), BF16),
        in_specs=[hbm] * 7,
        out_specs=hbm,
        scratch_shapes=scratch,
        compiler_params=pltpu.CompilerParams(
            collective_id=0, has_side_effects=True, vmem_limit_bytes=60 << 20
        ),
        name="layer",
    )(queries, key_input, value_input, gate_input, kv_state, norm_gain.reshape(1, 4096), out_weight.T)


def solution(mesh):
    in_specs = (
        P("seq", "head"),
        P("seq", "head"),
        P("seq", "head"),
        P("seq", "head"),
        P("head", None, None),
        P(),
        P("head", "seq"),
    )
    out_specs = P(("seq", "head"), None)
    return jax.shard_map(shards, mesh=mesh, in_specs=in_specs, out_specs=out_specs, check_vma=False)
```
